32 devices in a mesh: groups: 1, fsdp: 8 (over z, y), seq: 4 (over x, core), sub: 1.
Axes of the slice: x: 2, y: 2, z: 4, core: 2. Of those that a mesh axis runs over, the one named last changes fastest.
Arguments:
- tokens: bfloat16 [8, 1, 4, 128, 2048], P(('groups', 'fsdp'), 'sub', 'seq'), may hold values from -6 to 6
- frame_valid: int32 [8, 1, 4], P(('groups', 'fsdp'), 'sub'), may hold values from 0 to 1, as said below
- w_qkv: bfloat16 [2048, 3, 2048], P('fsdp', None, 'seq'), may hold values from -0.1875 to 0.1875
- w_out: bfloat16 [2048, 2048], P('seq', 'fsdp'), may hold values from -0.125 to 0.125
- w_act: bfloat16 [2048, 8192], P(None, 'fsdp'), may hold values from -0.125 to 0.125
- class_table: int32 [8192], P('fsdp'), may hold values from 0 to 120
- cam_bias: float32 [121], replicated, may hold values from -4 to 4
Outputs:
- hidden: bfloat16 [8, 1, 4, 128, 2048], P(('groups', 'fsdp'), 'sub', 'seq')
- logits: float32 [8, 1, 4, 8192], P('groups', 'sub', 'seq', 'fsdp')
The draws below stay inside these ranges and needn't reach their ends.
Inputs may be any that keep to these rules, and one draw needn't show every extreme that they name: `frame_valid`: each window has at least one frame with value 1.
All inputs are finite; a program needn't handle non-finite values.
Results may differ from the reference program's by a relative error of at most 0.0058.
Values may be sent and summed in bfloat16 or wider, within the bound.
A program may use at most 128 MiB of HBM per device.

```python
import math
import jax
import jax.numpy as jnp
from jax import lax

D = 2048
H = 16
DH = 128
ACT = 8192
CAM = 121
FTOK = 128
FRAMES = 4
WF = 8
WS = 1


def draw_frame_valid(key, part):
    first_key, second_key = jax.random.split(jax.random.fold_in(key, 4711))
    coin_draw = jax.random.randint(first_key, (WF, WS, FRAMES), 0, 4)
    keep_flags = (coin_draw > 0).astype(jnp.int32)
    forced_frame = jax.random.randint(second_key, (WF, WS, 1), 0, FRAMES)
    frame_ids = jnp.arange(FRAMES, dtype=jnp.int32)[None, None, :]
    forced_flags = (frame_ids == forced_frame).astype(jnp.int32)
    return jnp.maximum(keep_flags, forced_flags)


def touch_ends(drawn, stream_key, least, top_value):
    place = [jax.random.randint(jax.random.fold_in(stream_key, axis), (), 0, length) for axis, length in enumerate(drawn.shape)]
    main_axis = drawn.shape.index(max(drawn.shape))
    beside = place[:main_axis] + [(place[main_axis] + 1) % drawn.shape[main_axis]] + place[main_axis + 1:]
    return drawn.at[tuple(place)].set(least).at[tuple(beside)].set(top_value)


def level_of(rng, shape, cuts, least, top_value):
    factor_of, own = 1.0, jax.random.fold_in(rng, 6)
    for dim, shards_of in cuts:
        draws = jnp.exp(jax.random.uniform(jax.random.fold_in(own, dim), (shards_of,), jnp.float32, least / len(cuts), top_value / len(cuts)))
        factor_of = factor_of * jnp.repeat(draws, shape[dim] // shards_of).reshape([-1 if axis == dim else 1 for axis in range(len(shape))])
    return factor_of


def bell_draw(key, dims, scale, reach, pieces=(), held_as=jnp.bfloat16):
    values = scale * jax.random.normal(key, dims, jnp.float32)
    if pieces:
        values = values * level_of(key, dims, pieces, -0.22, 0.18)
    return jnp.clip(values, -reach, reach).astype(held_as)


def setup_inputs(seed: int = 0, part: int = 0) -> dict:
    splits = jax.random.split(jax.random.key(seed), 8)
    own_keys = jax.random.split(jax.random.fold_in(splits[7], part), 8)
    tokens = bell_draw(own_keys[0], (WF, WS, FRAMES, FTOK, D), 1.0, 6.0, ((0, 8), (2, 4)))
    frame_valid = draw_frame_valid(jax.random.fold_in(jax.random.fold_in(splits[7], part), 71), part)
    w_qkv = bell_draw(splits[2], (D, 3, D), (D // 2) ** -0.5, 0.1875, ((0, 8), (2, 4)))
    w_out = bell_draw(splits[3], (D, D), D ** -0.5, 0.125, ((0, 4), (1, 8)))
    w_act = bell_draw(splits[4], (D, ACT), D ** -0.5, 0.125, ((1, 8),))
    class_table = touch_ends(jax.random.randint(splits[5], (ACT,), 0, CAM), jax.random.fold_in(splits[5], 1), 0, CAM - 1).astype(jnp.int32)
    cam_bias = bell_draw(splits[6], (CAM,), 1.0, 4.0, (), jnp.float32)
    return {"tokens": tokens, "frame_valid": frame_valid, "w_qkv": w_qkv, "w_out": w_out, "w_act": w_act, "class_table": class_table, "cam_bias": cam_bias}


def normalize(values):
    centre = lax.optimization_barrier(jnp.mean(values, axis=-1, keepdims=True))
    spread = lax.optimization_barrier(jnp.mean(jnp.square(values - centre), axis=-1, keepdims=True))
    return (values - centre) * lax.rsqrt(spread + 1e-05)

def reference(tokens, frame_valid, w_qkv, w_out, w_act, class_table, cam_bias):
    span_rows = FRAMES * FTOK
    flat_tokens = tokens.reshape(WF * WS, span_rows, D)
    flat_valid = frame_valid.reshape(WF * WS, FRAMES)
    weight_matrix = w_qkv.reshape(D, 3 * H * DH)
    score_scale = 1.0 / math.sqrt(DH)

    def one_window(window_pair):
        window_tokens, window_flags = window_pair
        normed = normalize(window_tokens.astype(jnp.float32)).astype(jnp.bfloat16)
        projected = jnp.dot(normed, weight_matrix, preferred_element_type=jnp.float32).astype(jnp.bfloat16)
        projected = lax.optimization_barrier(projected)
        projected = projected.reshape(span_rows, 3, H, DH).astype(jnp.float32)
        queries = projected[:, 0]
        keys_all = projected[:, 1]
        values_all = projected[:, 2]
        key_mask = jnp.repeat(window_flags.astype(jnp.float32), FTOK)
        scores = jnp.einsum('qhe,khe->hqk', queries, keys_all) * score_scale
        weights = jnp.exp(scores) * key_mask[None, None, :]
        totals = lax.optimization_barrier(jnp.sum(weights, axis=-1))
        rounded = lax.optimization_barrier(weights.astype(jnp.bfloat16)).astype(jnp.float32)
        mixed_heads = jnp.einsum('hqk,khe->hqe', rounded, values_all) / totals[:, :, None]
        mixed_heads = jnp.transpose(mixed_heads, (1, 0, 2)).reshape(span_rows, H * DH).astype(jnp.bfloat16)
        branch = jnp.dot(mixed_heads, w_out, preferred_element_type=jnp.float32)
        return (window_tokens.astype(jnp.float32) + branch).astype(jnp.bfloat16)
    hidden_flat = lax.map(one_window, (flat_tokens, flat_valid))
    hidden = hidden_flat.reshape(WF, WS, FRAMES, FTOK, D)
    hidden_wide = lax.optimization_barrier(hidden).astype(jnp.float32)
    pooled = normalize(lax.optimization_barrier(jnp.mean(hidden_wide, axis=3))).astype(jnp.bfloat16)
    pooled = pooled.reshape(WF * WS * FRAMES, D)
    head_scores = jnp.dot(pooled, w_act, preferred_element_type=jnp.float32)
    bias_cols = cam_bias[class_table]
    logits = (head_scores + bias_cols[None, :]).reshape(WF, WS, FRAMES, ACT)
    return (hidden, logits)
```

```python
import functools
import math

import jax
import jax.numpy as jnp
from jax import lax
from jax.experimental import pallas as pl
from jax.experimental.pallas import tpu as pltpu
from jax.sharding import PartitionSpec as P

DH = 128
PAIR = 2
UP, DOWN, ACROSS = 0, 1, 2
LINE_QKV, PAIR_QKV, LINE_OUT = 0, 1, 2
F32 = jnp.float32
BF16 = jnp.bfloat16


def normalize(values):
    centre = jnp.mean(values, axis=-1, keepdims=True)
    shifted = values - centre
    spread = jnp.mean(jnp.square(shifted), axis=-1, keepdims=True)
    return shifted * lax.rsqrt(spread + 1e-05)


def layer_kernel(
    shards, seqs,
    tok_in, valid_ref, qkv_in, out_in, act_in, table_ref, bias_ref,
    hidden_ref, logits_ref,
    tok, nrm, own_tok, wz, wy, wo, act, acc_z, acc_y, proj, att, own_part,
    part_out, part_in, hid, col_sum, row_tile, pool_tile, pool_wide, pool_rows, bias_row,
    local_sem, send_sem, recv_sem, tok_send, tok_recv, part_send, part_recv, pool_send, pool_recv,
):
    f = lax.axis_index("fsdp")
    s = lax.axis_index("seq")
    length = shards // PAIR
    a = f // PAIR
    b = f % PAIR
    rows = tok.shape[1]
    depth = nrm.shape[2]
    cols = wo.shape[2]
    z_cols = wz.shape[2]
    width = proj.shape[1] // 3
    heads = width // DH
    model = tok.shape[2]
    bufs = (wz, wy, wo)

    local = [
        pltpu.make_async_copy(tok_in, tok.at[0], local_sem.at[0]),
        pltpu.make_async_copy(qkv_in.at[:, pl.ds(0, z_cols)], wz.at[f], local_sem.at[1]),
        pltpu.make_async_copy(
            qkv_in.at[:, pl.ds(z_cols, wy.shape[2])], wy.at[f], local_sem.at[2]
        ),
        pltpu.make_async_copy(out_in, wo.at[f], local_sem.at[3]),
        pltpu.make_async_copy(act_in, act, local_sem.at[4]),
    ]
    for copy in local:
        copy.start()

    barrier = pltpu.get_barrier_semaphore()
    for k in range(1, shards):
        pl.semaphore_signal(barrier, inc=1, device_id={"fsdp": lax.rem(f + k, shards)},
                            device_id_type=pl.DeviceIdType.MESH)
    for k in range(1, seqs):
        pl.semaphore_signal(barrier, inc=1, device_id={"seq": lax.rem(s + k, seqs)},
                            device_id_type=pl.DeviceIdType.MESH)

    def shard_copy(kind, origin, way):
        if way == UP:
            target = lax.rem(f + PAIR, shards)
        elif way == DOWN:
            target = lax.rem(f + shards - PAIR, shards)
        else:
            target = a * PAIR + (1 - b)
        return pltpu.make_async_remote_copy(
            src_ref=bufs[kind].at[origin],
            dst_ref=bufs[kind].at[origin],
            send_sem=send_sem.at[way, kind, origin],
            recv_sem=recv_sem.at[kind, origin],
            device_id={"fsdp": target},
            device_id_type=pl.DeviceIdType.MESH,
        )

    def arrived(kind, origin):
        shard_copy(kind, origin, ACROSS).wait_recv()

    def send_up(kind, origin):
        @pl.when(a < length - 1)
        def _():
            shard_copy(kind, origin, UP).start()

    def send_down(kind, origin):
        @pl.when(a > 0)
        def _():
            shard_copy(kind, origin, DOWN).start()

    def at_distance(d, act_on):
        @pl.when(a - d >= 0)
        def _():
            act_on(0, a - d)

        @pl.when(jnp.logical_and(a + d < length, d > 0))
        def _():
            act_on(1, a + d)

    def tok_copy(k):
        return pltpu.make_async_remote_copy(
            src_ref=tok.at[0],
            dst_ref=tok.at[seqs - k],
            send_sem=tok_send.at[k],
            recv_sem=tok_recv.at[seqs - k],
            device_id={"seq": lax.rem(s + k, seqs)},
            device_id_type=pl.DeviceIdType.MESH,
        )

    for copy in local[:4]:
        copy.wait()
    pl.semaphore_wait(barrier, shards - 1 + seqs - 1)

    shard_copy(PAIR_QKV, f, ACROSS).start()
    shard_copy(LINE_QKV, f, ACROSS).start()
    send_up(LINE_QKV, f)
    send_down(LINE_QKV, f)
    for k in range(1, seqs):
        tok_copy(k).start()

    def norm_slot(k):
        step = 32

        def piece(i, carry):
            part = pl.ds(pl.multiple_of(i * step, step), step)
            values = normalize(tok[k, part, :].astype(F32)).astype(BF16)
            dest = pl.ds(pl.multiple_of(k * rows + i * step, step), step)
            for g in range(shards):
                nrm[g, dest, :] = values[:, g * depth:(g + 1) * depth]
            return carry

        lax.fori_loop(0, rows // step, piece, 0)

    norm_slot(0)
    for g in range(shards):
        own_tok[g] = tok[0, :, g * cols:(g + 1) * cols]
    table = table_ref[...]
    bins = bias_ref.shape[1]
    onehot = (lax.broadcasted_iota(jnp.int32, (bins, table.shape[1]), 0) == table).astype(F32)
    bias_row[...] = jnp.dot(
        bias_ref[...], onehot, preferred_element_type=F32, precision=lax.Precision.HIGHEST
    )
    acc_z[...] = jnp.zeros_like(acc_z)
    acc_y[...] = jnp.zeros_like(acc_y)

    half = acc_z.shape[0] // 2

    def add_z(origin):
        def piece(i, carry):
            part = pl.ds(pl.multiple_of(i * half, half), half)
            acc_z[part, :] += jnp.dot(nrm[origin, part, :], wz[origin],
                                      preferred_element_type=F32)
            return carry

        lax.fori_loop(0, 2, piece, 0)

    def add_y(origin):
        acc_y[...] += jnp.dot(nrm[origin], wy[origin], preferred_element_type=F32)

    def line_forward(kind, d):
        def forward(side, o):
            origin = o * PAIR + b
            arrived(kind, origin)
            if side == 0:
                send_up(kind, origin)
            else:
                send_down(kind, origin)
            shard_copy(kind, origin, ACROSS).start()

        at_distance(d, forward)

    turn = max(length - 2, 1)

    def line_step(d, carry):
        line_forward(LINE_QKV, d)

        @pl.when(d == turn)
        def _():
            send_up(PAIR_QKV, f)
            send_down(PAIR_QKV, f)
            other = a * PAIR + (1 - b)
            arrived(PAIR_QKV, other)
            send_up(PAIR_QKV, other)
            send_down(PAIR_QKV, other)

        @pl.when(d == 1)
        def _():
            for k in range(1, seqs):
                tok_copy(seqs - k).wait_recv()
                norm_slot(k)
            add_z(f)

        at_distance(d, lambda side, o: add_z(o * PAIR + b))
        return carry

    lax.fori_loop(1, length, line_step, 0)
    shard_copy(LINE_OUT, f, ACROSS).start()

    add_y(f)
    add_y(a * PAIR + (1 - b))

    def across_z(d):
        def use(side, o):
            origin = o * PAIR + (1 - b)
            arrived(LINE_QKV, origin)
            add_z(origin)

        at_distance(d, use)

    def pair_step(d, carry):
        for column in (b, 1 - b):
            def forward(side, o):
                origin = o * PAIR + column
                arrived(PAIR_QKV, origin)
                if side == 0:
                    send_up(PAIR_QKV, origin)
                else:
                    send_down(PAIR_QKV, origin)

            at_distance(d, forward)

        @pl.when(d == turn)
        def _():
            send_up(LINE_OUT, f)
            send_down(LINE_OUT, f)

        def use(side, o):
            add_y(o * PAIR)
            add_y(o * PAIR + 1)

        at_distance(d, use)
        across_z(d - 1)
        return carry

    lax.fori_loop(1, length, pair_step, 0)
    across_z(length - 1)

    proj[:, 0:z_cols] = acc_z[...].astype(BF16)
    proj[:, z_cols:] = acc_y[...].astype(BF16)
    scale = 1.0 / math.sqrt(DH)

    def head_step(h, carry):
        start = pl.multiple_of(h * DH, DH)
        query = proj[:, pl.ds(start, DH)]
        key = proj[:, pl.ds(width + start, DH)]
        value = proj[:, pl.ds(2 * width + start, DH)]
        total = None
        mixed = None
        for k in range(seqs):
            part = slice(k * rows, (k + 1) * rows)
            score = lax.dot_general(query, key[part], (((1,), (1,)), ((), ())),
                                    preferred_element_type=F32)
            keep = valid_ref[0, lax.rem(s + k, seqs)].astype(F32)
            weight = jnp.exp(score * scale) * keep
            part_total = jnp.sum(weight, axis=-1, keepdims=True)
            part_mixed = jnp.dot(weight.astype(BF16), value[part], preferred_element_type=F32)
            total = part_total if total is None else total + part_total
            mixed = part_mixed if mixed is None else mixed + part_mixed
        att[:, pl.ds(start, DH)] = (mixed / total).astype(BF16)
        return carry

    lax.fori_loop(0, heads, head_step, 0)

    def part_copy(k, block):
        return pltpu.make_async_remote_copy(
            src_ref=part_out.at[k - 1, block],
            dst_ref=part_in.at[seqs - k - 1, block],
            send_sem=part_send.at[k - 1, block],
            recv_sem=part_recv.at[seqs - k - 1, block],
            device_id={"seq": lax.rem(s + k, seqs)},
            device_id_type=pl.DeviceIdType.MESH,
        )

    def out_block(block):
        product = jnp.dot(att[...], wo[block], preferred_element_type=F32)
        for k in range(1, seqs):
            part_out[k - 1, block] = product[k * rows:(k + 1) * rows].astype(BF16)
        own_part[block] = product[0:rows]
        for k in range(1, seqs):
            part_copy(k, block).start()

    out_block(f)

    def across_out(d):
        def use(side, o):
            origin = o * PAIR + (1 - b)
            arrived(LINE_OUT, origin)
            out_block(origin)

        at_distance(d, use)

    def out_step(d, carry):
        line_forward(LINE_OUT, d)
        at_distance(d, lambda side, o: out_block(o * PAIR + b))
        across_out(d - 1)
        return carry

    lax.fori_loop(1, length, out_step, 0)
    across_out(length - 1)

    def finish(block, carry):
        total = own_part[block]
        for k in range(1, seqs):
            part_copy(seqs - k, block).wait_recv()
            total = total + part_in[k - 1, block].astype(F32)
        rounded = (own_tok[block].astype(F32) + total).astype(BF16)
        hid[block] = rounded
        col_sum[block] = jnp.sum(rounded.astype(F32), axis=0, keepdims=True)
        return carry

    lax.fori_loop(0, shards, finish, 0)

    pooled = normalize(
        jnp.concatenate([col_sum[g] for g in range(shards)], axis=-1) * (1.0 / rows)
    )
    lanes = row_tile.shape[1]
    for i in range(model // lanes):
        row_tile[i:i + 1, :] = pooled[:, i * lanes:(i + 1) * lanes]
    pool_tile[f] = row_tile[...].astype(BF16)

    def pool_copy(k):
        target = lax.rem(f + k, shards)
        return pltpu.make_async_remote_copy(
            src_ref=pool_tile.at[f],
            dst_ref=pool_tile.at[f],
            send_sem=pool_send.at[k],
            recv_sem=pool_recv.at[k],
            device_id={"fsdp": target},
            device_id_type=pl.DeviceIdType.MESH,
        )

    for k in range(1, shards):
        pool_copy(k).start()
    for g in range(shards):
        hidden_ref[:, g * cols:(g + 1) * cols] = hid[g]
    local[4].wait()

    for k in range(1, seqs):
        tok_copy(k).wait_send()

    def drain(o, carry):
        own = o * PAIR + b
        other = o * PAIR + (1 - b)
        for kind in (LINE_QKV, LINE_OUT):
            shard_copy(kind, own, ACROSS).wait_send()

        @pl.when(jnp.logical_and(o <= a, a < length - 1))
        def _():
            for kind in (LINE_QKV, LINE_OUT, PAIR_QKV):
                shard_copy(kind, own, UP).wait_send()
            shard_copy(PAIR_QKV, other, UP).wait_send()

        @pl.when(jnp.logical_and(o >= a, a > 0))
        def _():
            for kind in (LINE_QKV, LINE_OUT, PAIR_QKV):
                shard_copy(kind, own, DOWN).wait_send()
            shard_copy(PAIR_QKV, other, DOWN).wait_send()

        return carry

    lax.fori_loop(0, length, drain, 0)
    shard_copy(PAIR_QKV, f, ACROSS).wait_send()

    def drain_parts(block, carry):
        for k in range(1, seqs):
            part_copy(k, block).wait_send()
        return carry

    lax.fori_loop(0, shards, drain_parts, 0)

    for k in range(1, shards):
        pool_copy(k).wait_recv()
    pool_wide[...] = pool_tile[...].astype(F32)
    for i in range(model // lanes):
        pool_rows[:, i * lanes:(i + 1) * lanes] = pool_wide[:, i, :]
    logits_ref[...] = (
        jnp.dot(pool_rows[...].astype(BF16), act[...], preferred_element_type=F32)
        + bias_row[...]
    )
    for k in range(1, shards):
        pool_copy(k).wait_send()


def per_device(shards, seqs, tokens, frame_valid, w_qkv, w_out, w_act, class_table, cam_bias):
    rows, model = tokens.shape[3], tokens.shape[4]
    depth, width = w_qkv.shape[0], w_qkv.shape[2]
    cols, classes = w_out.shape[1], w_act.shape[1]
    span = seqs * rows
    y_cols = 3 * width // 4
    z_cols = 3 * width - y_cols
    lanes = 128
    any_spec = pl.BlockSpec(memory_space=pl.ANY)
    vmem_spec = pl.BlockSpec(memory_space=pltpu.VMEM)
    hidden, logits = pl.pallas_call(
        functools.partial(layer_kernel, shards, seqs),
        out_shape=(
            jax.ShapeDtypeStruct((rows, model), BF16),
            jax.ShapeDtypeStruct((shards, classes), F32),
        ),
        in_specs=[
            any_spec,
            pl.BlockSpec(memory_space=pltpu.SMEM),
            any_spec, any_spec, any_spec, vmem_spec, vmem_spec,
        ],
        out_specs=(vmem_spec, vmem_spec),
        scratch_shapes=[
            pltpu.VMEM((seqs, rows, model), BF16),
            pltpu.VMEM((shards, span, depth), BF16),
            pltpu.VMEM((shards, rows, cols), BF16),
            pltpu.VMEM((shards, depth, z_cols), BF16),
            pltpu.VMEM((shards, depth, y_cols), BF16),
            pltpu.VMEM((shards, width, cols), BF16),
            pltpu.VMEM((model, classes), BF16),
            pltpu.VMEM((span, z_cols), F32),
            pltpu.VMEM((span, y_cols), F32),
            pltpu.VMEM((span, 3 * width), BF16),
            pltpu.VMEM((span, width), BF16),
            pltpu.VMEM((shards, rows, cols), F32),
            pltpu.VMEM((seqs - 1, shards, rows, cols), BF16),
            pltpu.VMEM((seqs - 1, shards, rows, cols), BF16),
            pltpu.VMEM((shards, rows, cols), BF16),
            pltpu.VMEM((shards, 1, cols), F32),
            pltpu.VMEM((model // lanes, lanes), F32),
            pltpu.VMEM((shards, model // lanes, lanes), BF16),
            pltpu.VMEM((shards, model // lanes, lanes), F32),
            pltpu.VMEM((shards, model), F32),
            pltpu.VMEM((1, classes), F32),
            pltpu.SemaphoreType.DMA((5,)),
            pltpu.SemaphoreType.DMA((3, 3, shards)),
            pltpu.SemaphoreType.DMA((3, shards)),
            pltpu.SemaphoreType.DMA((seqs,)),
            pltpu.SemaphoreType.DMA((seqs,)),
            pltpu.SemaphoreType.DMA((seqs - 1, shards)),
            pltpu.SemaphoreType.DMA((seqs - 1, shards)),
            pltpu.SemaphoreType.DMA((shards,)),
            pltpu.SemaphoreType.DMA((shards,)),
        ],
        compiler_params=pltpu.CompilerParams(
            collective_id=0, has_side_effects=True, vmem_limit_bytes=60 * 1024 * 1024
        ),
        name="layer",
    )(
        tokens.reshape(rows, model),
        frame_valid.reshape(1, seqs),
        w_qkv.reshape(depth, 3 * width),
        w_out,
        w_act,
        class_table.reshape(1, classes),
        cam_bias.reshape(1, cam_bias.shape[0]),
    )
    return (
        hidden.reshape(1, 1, 1, rows, model),
        logits.reshape(shards, 1, 1, classes),
    )


def solution(mesh):
    in_specs = (
        P(("groups", "fsdp"), "sub", "seq", None, None),
        P(("groups", "fsdp"), "sub", None),
        P("fsdp", None, "seq"),
        P("seq", "fsdp"),
        P(None, "fsdp"),
        P("fsdp"),
        P(),
    )
    out_specs = (P(("groups", "fsdp"), "sub", "seq", None, None), P("groups", "sub", "seq", "fsdp"))
    body = functools.partial(per_device, mesh.shape["fsdp"], mesh.shape["seq"])
    return jax.shard_map(
        body, mesh=mesh, in_specs=in_specs, out_specs=out_specs, check_vma=False
    )
```

```python
import functools
import math

import jax
import jax.numpy as jnp
from jax import lax
from jax.experimental import pallas as pl
from jax.experimental.pallas import tpu as pltpu
from jax.sharding import PartitionSpec as P

DH = 128
PAIR = 2
UP, DOWN, ACROSS = 0, 1, 2
LINE_QKV, PAIR_QKV, LINE_OUT = 0, 1, 2
F32 = jnp.float32
BF16 = jnp.bfloat16


def normalize(values):
    centre = jnp.mean(values, axis=-1, keepdims=True)
    shifted = values - centre
    spread = jnp.mean(jnp.square(shifted), axis=-1, keepdims=True)
    return shifted * lax.rsqrt(spread + 1e-05)


def layer_kernel(
    shards, seqs,
    tok_in, valid_ref, qkv_in, out_in, act_in, table_ref, bias_ref,
    hidden_ref, logits_ref,
    tok, nrm, own_tok, wz, wy, wo, act, acc_z, acc_y, proj, att, own_part,
    part_out, part_in, hid, col_sum, row_tile, pool_tile, pool_wide, pool_rows, bias_row, hidden_tile,
    local_sem, send_sem, recv_sem, tok_send, tok_recv, part_send, part_recv, pool_send, pool_recv,
):
    f = lax.axis_index("fsdp")
    s = lax.axis_index("seq")
    length = shards // PAIR
    a = f // PAIR
    b = f % PAIR
    rows = tok.shape[1]
    depth = nrm.shape[2]
    cols = wo.shape[2]
    z_cols = wz.shape[2]
    width = proj.shape[1] // 3
    heads = width // DH
    model = tok.shape[2]
    bufs = (wz, wy, wo)

    local = [
        pltpu.make_async_copy(tok_in, tok.at[0], local_sem.at[0]),
        pltpu.make_async_copy(
            qkv_in.at[0], wz.at[f, :, pl.ds(0, width)], local_sem.at[1]
        ),
        pltpu.make_async_copy(
            qkv_in.at[1], wz.at[f, :, pl.ds(width, width)], local_sem.at[2]
        ),
        pltpu.make_async_copy(
            qkv_in.at[2, :, pl.ds(0, z_cols - 2 * width)],
            wz.at[f, :, pl.ds(2 * width, z_cols - 2 * width)],
            local_sem.at[3],
        ),
        pltpu.make_async_copy(
            qkv_in.at[2, :, pl.ds(z_cols - 2 * width, wy.shape[2])], wy.at[f], local_sem.at[4]
        ),
        pltpu.make_async_copy(out_in, wo.at[f], local_sem.at[5]),
        pltpu.make_async_copy(act_in, act, local_sem.at[6]),
    ]
    hidden_copy = pltpu.make_async_copy(hidden_tile, hidden_ref, local_sem.at[7])
    for copy in local:
        copy.start()

    barrier = pltpu.get_barrier_semaphore()
    for k in range(1, shards):
        pl.semaphore_signal(barrier, inc=1, device_id={"fsdp": lax.rem(f + k, shards)},
                            device_id_type=pl.DeviceIdType.MESH)
    for k in range(1, seqs):
        pl.semaphore_signal(barrier, inc=1, device_id={"seq": lax.rem(s + k, seqs)},
                            device_id_type=pl.DeviceIdType.MESH)

    def shard_copy(kind, origin, way):
        if way == UP:
            target = lax.rem(f + PAIR, shards)
        elif way == DOWN:
            target = lax.rem(f + shards - PAIR, shards)
        else:
            target = a * PAIR + (1 - b)
        return pltpu.make_async_remote_copy(
            src_ref=bufs[kind].at[origin],
            dst_ref=bufs[kind].at[origin],
            send_sem=send_sem.at[way, kind, origin],
            recv_sem=recv_sem.at[kind, origin],
            device_id={"fsdp": target},
            device_id_type=pl.DeviceIdType.MESH,
        )

    def arrived(kind, origin):
        shard_copy(kind, origin, ACROSS).wait_recv()

    def send_up(kind, origin):
        @pl.when(a < length - 1)
        def _():
            shard_copy(kind, origin, UP).start()

    def send_down(kind, origin):
        @pl.when(a > 0)
        def _():
            shard_copy(kind, origin, DOWN).start()

    def at_distance(d, act_on):
        @pl.when(a - d >= 0)
        def _():
            act_on(0, a - d)

        @pl.when(jnp.logical_and(a + d < length, d > 0))
        def _():
            act_on(1, a + d)

    def tok_copy(k):
        return pltpu.make_async_remote_copy(
            src_ref=tok.at[0],
            dst_ref=tok.at[seqs - k],
            send_sem=tok_send.at[k],
            recv_sem=tok_recv.at[seqs - k],
            device_id={"seq": lax.rem(s + k, seqs)},
            device_id_type=pl.DeviceIdType.MESH,
        )

    for copy in local[:6]:
        copy.wait()
    pl.semaphore_wait(barrier, shards - 1 + seqs - 1)

    shard_copy(PAIR_QKV, f, ACROSS).start()
    shard_copy(LINE_QKV, f, ACROSS).start()
    send_up(LINE_QKV, f)
    send_down(LINE_QKV, f)
    for k in range(1, seqs):
        tok_copy(k).start()

    def norm_slot(k):
        step = 32

        def piece(i, carry):
            part = pl.ds(pl.multiple_of(i * step, step), step)
            values = normalize(tok[k, part, :].astype(F32)).astype(BF16)
            dest = pl.ds(pl.multiple_of(k * rows + i * step, step), step)
            for g in range(shards):
                nrm[g, dest, :] = values[:, g * depth:(g + 1) * depth]
            return carry

        lax.fori_loop(0, rows // step, piece, 0)

    norm_slot(0)
    for g in range(shards):
        own_tok[g] = tok[0, :, g * cols:(g + 1) * cols]
    table = table_ref[...]
    bins = bias_ref.shape[1]
    onehot = (lax.broadcasted_iota(jnp.int32, (bins, table.shape[1]), 0) == table).astype(F32)
    bias_row[...] = jnp.dot(
        bias_ref[...], onehot, preferred_element_type=F32, precision=lax.Precision.HIGHEST
    )
    acc_z[...] = jnp.zeros_like(acc_z)
    acc_y[...] = jnp.zeros_like(acc_y)

    half = acc_z.shape[0] // 2

    def add_z(origin):
        def piece(i, carry):
            part = pl.ds(pl.multiple_of(i * half, half), half)
            acc_z[part, :] += jnp.dot(nrm[origin, part, :], wz[origin],
                                      preferred_element_type=F32)
            return carry

        lax.fori_loop(0, 2, piece, 0)

    def add_y(origin):
        acc_y[...] += jnp.dot(nrm[origin], wy[origin], preferred_element_type=F32)

    def line_forward(kind, d):
        def forward(side, o):
            origin = o * PAIR + b
            arrived(kind, origin)
            if side == 0:
                send_up(kind, origin)
            else:
                send_down(kind, origin)
            shard_copy(kind, origin, ACROSS).start()

        at_distance(d, forward)

    turn = max(length - 2, 1)

    def line_step(d, carry):
        line_forward(LINE_QKV, d)

        @pl.when(d == turn)
        def _():
            send_up(PAIR_QKV, f)
            send_down(PAIR_QKV, f)
            other = a * PAIR + (1 - b)
            arrived(PAIR_QKV, other)
            send_up(PAIR_QKV, other)
            send_down(PAIR_QKV, other)

        @pl.when(d == 1)
        def _():
            for k in range(1, seqs):
                tok_copy(seqs - k).wait_recv()
                norm_slot(k)
            add_z(f)

        at_distance(d, lambda side, o: add_z(o * PAIR + b))
        return carry

    lax.fori_loop(1, length, line_step, 0)
    shard_copy(LINE_OUT, f, ACROSS).start()

    add_y(f)
    add_y(a * PAIR + (1 - b))

    def across_z(d):
        def use(side, o):
            origin = o * PAIR + (1 - b)
            arrived(LINE_QKV, origin)
            add_z(origin)

        at_distance(d, use)

    def pair_step(d, carry):
        for column in (b, 1 - b):
            def forward(side, o):
                origin = o * PAIR + column
                arrived(PAIR_QKV, origin)
                if side == 0:
                    send_up(PAIR_QKV, origin)
                else:
                    send_down(PAIR_QKV, origin)

            at_distance(d, forward)

        @pl.when(d == turn)
        def _():
            send_up(LINE_OUT, f)
            send_down(LINE_OUT, f)

        def use(side, o):
            add_y(o * PAIR)
            add_y(o * PAIR + 1)

        at_distance(d, use)
        across_z(d - 1)
        return carry

    lax.fori_loop(1, length, pair_step, 0)
    across_z(length - 1)

    proj[:, 0:z_cols] = acc_z[...].astype(BF16)
    proj[:, z_cols:] = acc_y[...].astype(BF16)
    scale = 1.0 / math.sqrt(DH)

    def head_step(h, carry):
        start = pl.multiple_of(h * DH, DH)
        query = proj[:, pl.ds(start, DH)]
        key = proj[:, pl.ds(width + start, DH)]
        value = proj[:, pl.ds(2 * width + start, DH)]
        total = None
        mixed = None
        for k in range(seqs):
            part = slice(k * rows, (k + 1) * rows)
            score = lax.dot_general(query, key[part], (((1,), (1,)), ((), ())),
                                    preferred_element_type=F32)
            keep = valid_ref[0, lax.rem(s + k, seqs)].astype(F32)
            weight = jnp.exp(score * scale) * keep
            part_total = jnp.sum(weight, axis=-1, keepdims=True)
            part_mixed = jnp.dot(weight.astype(BF16), value[part], preferred_element_type=F32)
            total = part_total if total is None else total + part_total
            mixed = part_mixed if mixed is None else mixed + part_mixed
        att[:, pl.ds(start, DH)] = (mixed / total).astype(BF16)
        return carry

    lax.fori_loop(0, heads, head_step, 0)

    def part_copy(k, block):
        return pltpu.make_async_remote_copy(
            src_ref=part_out.at[k - 1, block],
            dst_ref=part_in.at[seqs - k - 1, block],
            send_sem=part_send.at[k - 1, block],
            recv_sem=part_recv.at[seqs - k - 1, block],
            device_id={"seq": lax.rem(s + k, seqs)},
            device_id_type=pl.DeviceIdType.MESH,
        )

    def out_block(block):
        product = jnp.dot(att[...], wo[block], preferred_element_type=F32)
        for k in range(1, seqs):
            part_out[k - 1, block] = product[k * rows:(k + 1) * rows].astype(BF16)
        own_part[block] = product[0:rows]
        for k in range(1, seqs):
            part_copy(k, block).start()

    out_block(f)

    def across_out(d):
        def use(side, o):
            origin = o * PAIR + (1 - b)
            arrived(LINE_OUT, origin)
            out_block(origin)

        at_distance(d, use)

    def finish(block):
        total = own_part[block]
        for k in range(1, seqs):
            part_copy(seqs - k, block).wait_recv()
            total = total + part_in[k - 1, block].astype(F32)
        rounded = (own_tok[block].astype(F32) + total).astype(BF16)
        hid[block] = rounded
        col_sum[block] = jnp.sum(rounded.astype(F32), axis=0, keepdims=True)

    def finish_at(d, column):
        at_distance(d, lambda side, o: finish(o * PAIR + column))

    def out_step(d, carry):
        line_forward(LINE_OUT, d)
        at_distance(d, lambda side, o: out_block(o * PAIR + b))
        finish_at(d - 1, b)

        @pl.when(d >= 2)
        def _():
            finish_at(d - 2, 1 - b)

        across_out(d - 1)
        return carry

    lax.fori_loop(1, length, out_step, 0)
    finish_at(length - 1, b)
    finish_at(length - 2, 1 - b)
    across_out(length - 1)
    finish_at(length - 1, 1 - b)


    pooled = normalize(
        jnp.concatenate([col_sum[g] for g in range(shards)], axis=-1) * (1.0 / rows)
    )
    lanes = row_tile.shape[1]
    for i in range(model // lanes):
        row_tile[i:i + 1, :] = pooled[:, i * lanes:(i + 1) * lanes]
    pool_tile[f] = row_tile[...].astype(BF16)

    def pool_copy(k):
        target = lax.rem(f + k, shards)
        return pltpu.make_async_remote_copy(
            src_ref=pool_tile.at[f],
            dst_ref=pool_tile.at[f],
            send_sem=pool_send.at[k],
            recv_sem=pool_recv.at[k],
            device_id={"fsdp": target},
            device_id_type=pl.DeviceIdType.MESH,
        )

    for k in range(1, shards):
        pool_copy(k).start()
    for g in range(shards):
        hidden_tile[:, g * cols:(g + 1) * cols] = hid[g]
    hidden_copy.start()
    local[6].wait()

    for k in range(1, seqs):
        tok_copy(k).wait_send()

    def drain(o, carry):
        own = o * PAIR + b
        other = o * PAIR + (1 - b)
        for kind in (LINE_QKV, LINE_OUT):
            shard_copy(kind, own, ACROSS).wait_send()

        @pl.when(jnp.logical_and(o <= a, a < length - 1))
        def _():
            for kind in (LINE_QKV, LINE_OUT, PAIR_QKV):
                shard_copy(kind, own, UP).wait_send()
            shard_copy(PAIR_QKV, other, UP).wait_send()

        @pl.when(jnp.logical_and(o >= a, a > 0))
        def _():
            for kind in (LINE_QKV, LINE_OUT, PAIR_QKV):
                shard_copy(kind, own, DOWN).wait_send()
            shard_copy(PAIR_QKV, other, DOWN).wait_send()

        return carry

    lax.fori_loop(0, length, drain, 0)
    shard_copy(PAIR_QKV, f, ACROSS).wait_send()

    def drain_parts(block, carry):
        for k in range(1, seqs):
            part_copy(k, block).wait_send()
        return carry

    lax.fori_loop(0, shards, drain_parts, 0)

    for k in range(1, shards):
        pool_copy(k).wait_recv()
    pool_wide[...] = pool_tile[...].astype(F32)
    for i in range(model // lanes):
        pool_rows[:, i * lanes:(i + 1) * lanes] = pool_wide[:, i, :]
    logits_ref[...] = (
        jnp.dot(pool_rows[...].astype(BF16), act[...], preferred_element_type=F32)
        + bias_row[...]
    )
    for k in range(1, shards):
        pool_copy(k).wait_send()
    hidden_copy.wait()


def per_device(shards, seqs, tokens, frame_valid, w_qkv, w_out, w_act, class_table, cam_bias):
    rows, model = tokens.shape[3], tokens.shape[4]
    depth, width = w_qkv.shape[0], w_qkv.shape[2]
    cols, classes = w_out.shape[1], w_act.shape[1]
    span = seqs * rows
    y_cols = width // 2
    z_cols = 3 * width - y_cols
    lanes = 128
    any_spec = pl.BlockSpec(memory_space=pl.ANY)
    vmem_spec = pl.BlockSpec(memory_space=pltpu.VMEM)
    hidden, logits = pl.pallas_call(
        functools.partial(layer_kernel, shards, seqs),
        out_shape=(
            jax.ShapeDtypeStruct((rows, model), BF16),
            jax.ShapeDtypeStruct((shards, classes), F32),
        ),
        in_specs=[
            any_spec,
            pl.BlockSpec(memory_space=pltpu.SMEM),
            any_spec, any_spec, any_spec, vmem_spec, vmem_spec,
        ],
        out_specs=(any_spec, vmem_spec),
        scratch_shapes=[
            pltpu.VMEM((seqs, rows, model), BF16),
            pltpu.VMEM((shards, span, depth), BF16),
            pltpu.VMEM((shards, rows, cols), BF16),
            pltpu.VMEM((shards, depth, z_cols), BF16),
            pltpu.VMEM((shards, depth, y_cols), BF16),
            pltpu.VMEM((shards, width, cols), BF16),
            pltpu.VMEM((model, classes), BF16),
            pltpu.VMEM((span, z_cols), F32),
            pltpu.VMEM((span, y_cols), F32),
            pltpu.VMEM((span, 3 * width), BF16),
            pltpu.VMEM((span, width), BF16),
            pltpu.VMEM((shards, rows, cols), F32),
            pltpu.VMEM((seqs - 1, shards, rows, cols), BF16),
            pltpu.VMEM((seqs - 1, shards, rows, cols), BF16),
            pltpu.VMEM((shards, rows, cols), BF16),
            pltpu.VMEM((shards, 1, cols), F32),
            pltpu.VMEM((model // lanes, lanes), F32),
            pltpu.VMEM((shards, model // lanes, lanes), BF16),
            pltpu.VMEM((shards, model // lanes, lanes), F32),
            pltpu.VMEM((shards, model), F32),
            pltpu.VMEM((1, classes), F32),
            pltpu.VMEM((rows, model), BF16),
            pltpu.SemaphoreType.DMA((8,)),
            pltpu.SemaphoreType.DMA((3, 3, shards)),
            pltpu.SemaphoreType.DMA((3, shards)),
            pltpu.SemaphoreType.DMA((seqs,)),
            pltpu.SemaphoreType.DMA((seqs,)),
            pltpu.SemaphoreType.DMA((seqs - 1, shards)),
            pltpu.SemaphoreType.DMA((seqs - 1, shards)),
            pltpu.SemaphoreType.DMA((shards,)),
            pltpu.SemaphoreType.DMA((shards,)),
        ],
        compiler_params=pltpu.CompilerParams(
            collective_id=0, has_side_effects=True, vmem_limit_bytes=60 * 1024 * 1024
        ),
        name="layer",
    )(
        tokens.reshape(rows, model),
        frame_valid.reshape(1, seqs),
        jnp.transpose(w_qkv, (1, 0, 2)),
        w_out,
        w_act,
        class_table.reshape(1, classes),
        cam_bias.reshape(1, cam_bias.shape[0]),
    )
    return (
        hidden.reshape(1, 1, 1, rows, model),
        logits.reshape(shards, 1, 1, classes),
    )


def solution(mesh):
    in_specs = (
        P(("groups", "fsdp"), "sub", "seq", None, None),
        P(("groups", "fsdp"), "sub", None),
        P("fsdp", None, "seq"),
        P("seq", "fsdp"),
        P(None, "fsdp"),
        P("fsdp"),
        P(),
    )
    out_specs = (P(("groups", "fsdp"), "sub", "seq", None, None), P("groups", "sub", "seq", "fsdp"))
    body = functools.partial(per_device, mesh.shape["fsdp"], mesh.shape["seq"])
    return jax.shard_map(
        body, mesh=mesh, in_specs=in_specs, out_specs=out_specs, check_vma=False
    )
```

```python
import functools
import math

import jax
import jax.numpy as jnp
from jax import lax
from jax.experimental import pallas as pl
from jax.experimental.pallas import tpu as pltpu
from jax.sharding import PartitionSpec as P

DH = 128
PAIR = 2
UP, DOWN, ACROSS = 0, 1, 2
LINE_QKV, PAIR_QKV, LINE_OUT = 0, 1, 2
F32 = jnp.float32
BF16 = jnp.bfloat16


def normalize(values):
    centre = jnp.mean(values, axis=-1, keepdims=True)
    shifted = values - centre
    spread = jnp.mean(jnp.square(shifted), axis=-1, keepdims=True)
    return shifted * lax.rsqrt(spread + 1e-05)


def layer_kernel(
    shards, seqs,
    tok_in, valid_ref, qkv_in, out_in, act_in, table_ref, bias_ref,
    hidden_ref, logits_ref,
    tok, nrm, own_tok, wz, wy, wo, act, acc_z, acc_y, proj, att, own_part,
    mate_out, mate_in, part_out, part_in, hid, col_sum, row_tile, pool_tile, pool_wide, pool_rows, bias_row, hidden_tile,
    local_sem, send_sem, recv_sem, tok_send, tok_recv, mate_send, mate_recv, part_send, part_recv, pool_send, pool_recv,
):
    f = lax.axis_index("fsdp")
    s = lax.axis_index("seq")
    length = shards // PAIR
    a = f // PAIR
    b = f % PAIR
    rows = tok.shape[1]
    depth = nrm.shape[2]
    cols = wo.shape[2]
    z_cols = wz.shape[2]
    width = proj.shape[1] // 3
    heads = width // DH
    model = tok.shape[2]
    bufs = (wz, wy, wo)

    local = [
        pltpu.make_async_copy(tok_in, tok.at[0], local_sem.at[0]),
        pltpu.make_async_copy(
            qkv_in.at[0], wz.at[f, :, pl.ds(0, width)], local_sem.at[1]
        ),
        pltpu.make_async_copy(
            qkv_in.at[1], wz.at[f, :, pl.ds(width, width)], local_sem.at[2]
        ),
        pltpu.make_async_copy(
            qkv_in.at[2, :, pl.ds(0, z_cols - 2 * width)],
            wz.at[f, :, pl.ds(2 * width, z_cols - 2 * width)],
            local_sem.at[3],
        ),
        pltpu.make_async_copy(
            qkv_in.at[2, :, pl.ds(z_cols - 2 * width, wy.shape[2])], wy.at[f], local_sem.at[4]
        ),
        pltpu.make_async_copy(out_in, wo.at[f], local_sem.at[5]),
        pltpu.make_async_copy(act_in, act, local_sem.at[6]),
    ]
    hidden_copy = pltpu.make_async_copy(hidden_tile, hidden_ref, local_sem.at[7])
    for copy in local:
        copy.start()

    barrier = pltpu.get_barrier_semaphore()
    for k in range(1, shards):
        pl.semaphore_signal(barrier, inc=1, device_id={"fsdp": lax.rem(f + k, shards)},
                            device_id_type=pl.DeviceIdType.MESH)
    for k in range(1, seqs):
        pl.semaphore_signal(barrier, inc=1, device_id={"seq": lax.rem(s + k, seqs)},
                            device_id_type=pl.DeviceIdType.MESH)

    def shard_copy(kind, origin, way):
        if way == UP:
            target = lax.rem(f + PAIR, shards)
        elif way == DOWN:
            target = lax.rem(f + shards - PAIR, shards)
        else:
            target = a * PAIR + (1 - b)
        return pltpu.make_async_remote_copy(
            src_ref=bufs[kind].at[origin],
            dst_ref=bufs[kind].at[origin],
            send_sem=send_sem.at[way, kind, origin],
            recv_sem=recv_sem.at[kind, origin],
            device_id={"fsdp": target},
            device_id_type=pl.DeviceIdType.MESH,
        )

    def arrived(kind, origin):
        shard_copy(kind, origin, ACROSS).wait_recv()

    def send_up(kind, origin):
        @pl.when(a < length - 1)
        def _():
            shard_copy(kind, origin, UP).start()

    def send_down(kind, origin):
        @pl.when(a > 0)
        def _():
            shard_copy(kind, origin, DOWN).start()

    def at_distance(d, act_on):
        @pl.when(a - d >= 0)
        def _():
            act_on(0, a - d)

        @pl.when(jnp.logical_and(a + d < length, d > 0))
        def _():
            act_on(1, a + d)

    def tok_copy(k):
        return pltpu.make_async_remote_copy(
            src_ref=tok.at[0],
            dst_ref=tok.at[seqs - k],
            send_sem=tok_send.at[k],
            recv_sem=tok_recv.at[seqs - k],
            device_id={"seq": lax.rem(s + k, seqs)},
            device_id_type=pl.DeviceIdType.MESH,
        )

    for copy in local[:6]:
        copy.wait()
    pl.semaphore_wait(barrier, shards - 1 + seqs - 1)

    shard_copy(PAIR_QKV, f, ACROSS).start()
    shard_copy(LINE_QKV, f, ACROSS).start()
    send_up(LINE_QKV, f)
    send_down(LINE_QKV, f)
    for k in range(1, seqs):
        tok_copy(k).start()

    def norm_slot(k):
        step = 32

        def piece(i, carry):
            part = pl.ds(pl.multiple_of(i * step, step), step)
            values = normalize(tok[k, part, :].astype(F32)).astype(BF16)
            dest = pl.ds(pl.multiple_of(k * rows + i * step, step), step)
            for g in range(shards):
                nrm[g, dest, :] = values[:, g * depth:(g + 1) * depth]
            return carry

        lax.fori_loop(0, rows // step, piece, 0)

    norm_slot(0)
    for g in range(shards):
        own_tok[g] = tok[0, :, g * cols:(g + 1) * cols]
    table = table_ref[...]
    bins = bias_ref.shape[1]
    onehot = (lax.broadcasted_iota(jnp.int32, (bins, table.shape[1]), 0) == table).astype(F32)
    bias_row[...] = jnp.dot(
        bias_ref[...], onehot, preferred_element_type=F32, precision=lax.Precision.HIGHEST
    )
    acc_z[...] = jnp.zeros_like(acc_z)
    acc_y[...] = jnp.zeros_like(acc_y)

    half = acc_z.shape[0] // 2

    def add_z(origin):
        def piece(i, carry):
            part = pl.ds(pl.multiple_of(i * half, half), half)
            acc_z[part, :] += jnp.dot(nrm[origin, part, :], wz[origin],
                                      preferred_element_type=F32)
            return carry

        lax.fori_loop(0, 2, piece, 0)

    def add_y(origin):
        acc_y[...] += jnp.dot(nrm[origin], wy[origin], preferred_element_type=F32)

    def line_forward(kind, d):
        def forward(side, o):
            origin = o * PAIR + b
            arrived(kind, origin)
            if side == 0:
                send_up(kind, origin)
            else:
                send_down(kind, origin)
            shard_copy(kind, origin, ACROSS).start()

        at_distance(d, forward)

    turn = max(length - 2, 1)

    def line_step(d, carry):
        line_forward(LINE_QKV, d)

        @pl.when(d == turn)
        def _():
            send_up(PAIR_QKV, f)
            send_down(PAIR_QKV, f)
            other = a * PAIR + (1 - b)
            arrived(PAIR_QKV, other)
            send_up(PAIR_QKV, other)
            send_down(PAIR_QKV, other)

        @pl.when(d == 1)
        def _():
            for k in range(1, seqs):
                tok_copy(seqs - k).wait_recv()
                norm_slot(k)
            add_z(f)

        at_distance(d, lambda side, o: add_z(o * PAIR + b))
        return carry

    lax.fori_loop(1, length, line_step, 0)
    shard_copy(LINE_OUT, f, ACROSS).start()

    add_y(f)
    add_y(a * PAIR + (1 - b))

    def across_z(d):
        def use(side, o):
            origin = o * PAIR + (1 - b)
            arrived(LINE_QKV, origin)
            add_z(origin)

        at_distance(d, use)

    def pair_step(d, carry):
        for column in (b, 1 - b):
            def forward(side, o):
                origin = o * PAIR + column
                arrived(PAIR_QKV, origin)
                if side == 0:
                    send_up(PAIR_QKV, origin)
                else:
                    send_down(PAIR_QKV, origin)

            at_distance(d, forward)

        @pl.when(d == turn)
        def _():
            send_up(LINE_OUT, f)
            send_down(LINE_OUT, f)

        def use(side, o):
            add_y(o * PAIR)
            add_y(o * PAIR + 1)

        at_distance(d, use)
        across_z(d - 1)
        return carry

    lax.fori_loop(1, length, pair_step, 0)
    across_z(length - 1)

    proj[:, 0:z_cols] = acc_z[...].astype(BF16)
    proj[:, z_cols:] = acc_y[...].astype(BF16)
    scale = 1.0 / math.sqrt(DH)

    def head_step(h, carry):
        start = pl.multiple_of(h * DH, DH)
        query = proj[:, pl.ds(start, DH)]
        key = proj[:, pl.ds(width + start, DH)]
        value = proj[:, pl.ds(2 * width + start, DH)]
        total = None
        mixed = None
        for k in range(seqs):
            part = slice(k * rows, (k + 1) * rows)
            score = lax.dot_general(query, key[part], (((1,), (1,)), ((), ())),
                                    preferred_element_type=F32)
            keep = valid_ref[0, lax.rem(s + k, seqs)].astype(F32)
            weight = jnp.exp(score * scale) * keep
            part_total = jnp.sum(weight, axis=-1, keepdims=True)
            part_mixed = jnp.dot(weight.astype(BF16), value[part], preferred_element_type=F32)
            total = part_total if total is None else total + part_total
            mixed = part_mixed if mixed is None else mixed + part_mixed
        att[:, pl.ds(start, DH)] = (mixed / total).astype(BF16)
        return carry

    lax.fori_loop(0, heads, head_step, 0)

    odd = s % 2
    mate = s + 1 - 2 * odd
    folds = seqs // 2

    def mate_copy(block):
        return pltpu.make_async_remote_copy(
            src_ref=mate_out.at[block],
            dst_ref=mate_in.at[block],
            send_sem=mate_send.at[block],
            recv_sem=mate_recv.at[block],
            device_id={"seq": mate},
            device_id_type=pl.DeviceIdType.MESH,
        )

    def part_copy(j, block):
        return pltpu.make_async_remote_copy(
            src_ref=part_out.at[j - 1, block],
            dst_ref=part_in.at[folds - j - 1, block],
            send_sem=part_send.at[j - 1, block],
            recv_sem=part_recv.at[folds - j - 1, block],
            device_id={"seq": lax.rem(s + 2 * j, seqs)},
            device_id_type=pl.DeviceIdType.MESH,
        )

    def out_block(block):
        product = jnp.dot(att[...], wo[block], preferred_element_type=F32)

        def slot(k):
            return product[k * rows:(k + 1) * rows]

        for j in range(folds):
            mate_out[block, j] = jnp.where(
                odd == 0, slot(2 * j + 1), slot((2 * j - 1) % seqs)
            ).astype(BF16)
            own_part[block, j] = slot(2 * j)
        mate_copy(block).start()

    def fold_block(block):
        mate_copy(block).wait_recv()
        for j in range(1, folds):
            part_out[j - 1, block] = (
                own_part[block, j] + mate_in[block, j].astype(F32)
            ).astype(BF16)
            part_copy(j, block).start()

    out_block(f)
    fold_block(f)

    def across_out(d):
        def use(side, o):
            origin = o * PAIR + (1 - b)
            arrived(LINE_OUT, origin)
            out_block(origin)

        at_distance(d, use)
        at_distance(d, lambda side, o: fold_block(o * PAIR + (1 - b)))

    def finish(block):
        total = own_part[block, 0] + mate_in[block, 0].astype(F32)
        for j in range(1, folds):
            part_copy(folds - j, block).wait_recv()
            total = total + part_in[j - 1, block].astype(F32)
        rounded = (own_tok[block].astype(F32) + total).astype(BF16)
        hid[block] = rounded
        col_sum[block] = jnp.sum(rounded.astype(F32), axis=0, keepdims=True)

    def finish_at(d, column):
        at_distance(d, lambda side, o: finish(o * PAIR + column))

    def out_step(d, carry):
        line_forward(LINE_OUT, d)
        at_distance(d, lambda side, o: out_block(o * PAIR + b))
        at_distance(d, lambda side, o: fold_block(o * PAIR + b))
        finish_at(d - 1, b)

        @pl.when(d >= 2)
        def _():
            finish_at(d - 2, 1 - b)

        across_out(d - 1)
        return carry

    lax.fori_loop(1, length, out_step, 0)
    finish_at(length - 1, b)
    finish_at(length - 2, 1 - b)
    across_out(length - 1)
    finish_at(length - 1, 1 - b)


    pooled = normalize(
        jnp.concatenate([col_sum[g] for g in range(shards)], axis=-1) * (1.0 / rows)
    )
    lanes = row_tile.shape[1]
    for i in range(model // lanes):
        row_tile[i:i + 1, :] = pooled[:, i * lanes:(i + 1) * lanes]
    pool_tile[f] = row_tile[...].astype(BF16)

    def pool_copy(k):
        target = lax.rem(f + k, shards)
        return pltpu.make_async_remote_copy(
            src_ref=pool_tile.at[f],
            dst_ref=pool_tile.at[f],
            send_sem=pool_send.at[k],
            recv_sem=pool_recv.at[k],
            device_id={"fsdp": target},
            device_id_type=pl.DeviceIdType.MESH,
        )

    for k in range(1, shards):
        pool_copy(k).start()
    for g in range(shards):
        hidden_tile[:, g * cols:(g + 1) * cols] = hid[g]
    hidden_copy.start()
    local[6].wait()

    for k in range(1, seqs):
        tok_copy(k).wait_send()

    def drain(o, carry):
        own = o * PAIR + b
        other = o * PAIR + (1 - b)
        for kind in (LINE_QKV, LINE_OUT):
            shard_copy(kind, own, ACROSS).wait_send()

        @pl.when(jnp.logical_and(o <= a, a < length - 1))
        def _():
            for kind in (LINE_QKV, LINE_OUT, PAIR_QKV):
                shard_copy(kind, own, UP).wait_send()
            shard_copy(PAIR_QKV, other, UP).wait_send()

        @pl.when(jnp.logical_and(o >= a, a > 0))
        def _():
            for kind in (LINE_QKV, LINE_OUT, PAIR_QKV):
                shard_copy(kind, own, DOWN).wait_send()
            shard_copy(PAIR_QKV, other, DOWN).wait_send()

        return carry

    lax.fori_loop(0, length, drain, 0)
    shard_copy(PAIR_QKV, f, ACROSS).wait_send()

    def drain_parts(block, carry):
        mate_copy(block).wait_send()
        for j in range(1, folds):
            part_copy(j, block).wait_send()
        return carry

    lax.fori_loop(0, shards, drain_parts, 0)

    for k in range(1, shards):
        pool_copy(k).wait_recv()
    pool_wide[...] = pool_tile[...].astype(F32)
    for i in range(model // lanes):
        pool_rows[:, i * lanes:(i + 1) * lanes] = pool_wide[:, i, :]
    logits_ref[...] = (
        jnp.dot(pool_rows[...].astype(BF16), act[...], preferred_element_type=F32)
        + bias_row[...]
    )
    for k in range(1, shards):
        pool_copy(k).wait_send()
    hidden_copy.wait()


def per_device(shards, seqs, tokens, frame_valid, w_qkv, w_out, w_act, class_table, cam_bias):
    rows, model = tokens.shape[3], tokens.shape[4]
    depth, width = w_qkv.shape[0], w_qkv.shape[2]
    cols, classes = w_out.shape[1], w_act.shape[1]
    span = seqs * rows
    folds = seqs // 2
    y_cols = width // 2
    z_cols = 3 * width - y_cols
    lanes = 128
    any_spec = pl.BlockSpec(memory_space=pl.ANY)
    vmem_spec = pl.BlockSpec(memory_space=pltpu.VMEM)
    hidden, logits = pl.pallas_call(
        functools.partial(layer_kernel, shards, seqs),
        out_shape=(
            jax.ShapeDtypeStruct((rows, model), BF16),
            jax.ShapeDtypeStruct((shards, classes), F32),
        ),
        in_specs=[
            any_spec,
            pl.BlockSpec(memory_space=pltpu.SMEM),
            any_spec, any_spec, any_spec, vmem_spec, vmem_spec,
        ],
        out_specs=(any_spec, vmem_spec),
        scratch_shapes=[
            pltpu.VMEM((seqs, rows, model), BF16),
            pltpu.VMEM((shards, span, depth), BF16),
            pltpu.VMEM((shards, rows, cols), BF16),
            pltpu.VMEM((shards, depth, z_cols), BF16),
            pltpu.VMEM((shards, depth, y_cols), BF16),
            pltpu.VMEM((shards, width, cols), BF16),
            pltpu.VMEM((model, classes), BF16),
            pltpu.VMEM((span, z_cols), F32),
            pltpu.VMEM((span, y_cols), F32),
            pltpu.VMEM((span, 3 * width), BF16),
            pltpu.VMEM((span, width), BF16),
            pltpu.VMEM((shards, folds, rows, cols), F32),
            pltpu.VMEM((shards, folds, rows, cols), BF16),
            pltpu.VMEM((shards, folds, rows, cols), BF16),
            pltpu.VMEM((folds - 1, shards, rows, cols), BF16),
            pltpu.VMEM((folds - 1, shards, rows, cols), BF16),
            pltpu.VMEM((shards, rows, cols), BF16),
            pltpu.VMEM((shards, 1, cols), F32),
            pltpu.VMEM((model // lanes, lanes), F32),
            pltpu.VMEM((shards, model // lanes, lanes), BF16),
            pltpu.VMEM((shards, model // lanes, lanes), F32),
            pltpu.VMEM((shards, model), F32),
            pltpu.VMEM((1, classes), F32),
            pltpu.VMEM((rows, model), BF16),
            pltpu.SemaphoreType.DMA((8,)),
            pltpu.SemaphoreType.DMA((3, 3, shards)),
            pltpu.SemaphoreType.DMA((3, shards)),
            pltpu.SemaphoreType.DMA((seqs,)),
            pltpu.SemaphoreType.DMA((seqs,)),
            pltpu.SemaphoreType.DMA((shards,)),
            pltpu.SemaphoreType.DMA((shards,)),
            pltpu.SemaphoreType.DMA((folds - 1, shards)),
            pltpu.SemaphoreType.DMA((folds - 1, shards)),
            pltpu.SemaphoreType.DMA((shards,)),
            pltpu.SemaphoreType.DMA((shards,)),
        ],
        compiler_params=pltpu.CompilerParams(
            collective_id=0, has_side_effects=True, vmem_limit_bytes=60 * 1024 * 1024
        ),
        name="layer",
    )(
        tokens.reshape(rows, model),
        frame_valid.reshape(1, seqs),
        jnp.transpose(w_qkv, (1, 0, 2)),
        w_out,
        w_act,
        class_table.reshape(1, classes),
        cam_bias.reshape(1, cam_bias.shape[0]),
    )
    return (
        hidden.reshape(1, 1, 1, rows, model),
        logits.reshape(shards, 1, 1, classes),
    )


def solution(mesh):
    in_specs = (
        P(("groups", "fsdp"), "sub", "seq", None, None),
        P(("groups", "fsdp"), "sub", None),
        P("fsdp", None, "seq"),
        P("seq", "fsdp"),
        P(None, "fsdp"),
        P("fsdp"),
        P(),
    )
    out_specs = (P(("groups", "fsdp"), "sub", "seq", None, None), P("groups", "sub", "seq", "fsdp"))
    body = functools.partial(per_device, mesh.shape["fsdp"], mesh.shape["seq"])
    return jax.shard_map(
        body, mesh=mesh, in_specs=in_specs, out_specs=out_specs, check_vma=False
    )
```

```python
import functools
import math

import jax
import jax.numpy as jnp
from jax import lax
from jax.experimental import pallas as pl
from jax.experimental.pallas import tpu as pltpu
from jax.sharding import PartitionSpec as P

DH = 128
PAIR = 2
UP, DOWN, ACROSS = 0, 1, 2
LINE_QKV, PAIR_QKV, LINE_OUT = 0, 1, 2
F32 = jnp.float32
BF16 = jnp.bfloat16


def normalize(values):
    centre = jnp.mean(values, axis=-1, keepdims=True)
    shifted = values - centre
    spread = jnp.mean(jnp.square(shifted), axis=-1, keepdims=True)
    return shifted * lax.rsqrt(spread + 1e-05)


def layer_kernel(
    shards, seqs,
    tok_in, valid_ref, qkv_in, out_in, act_in, table_ref, bias_ref,
    hidden_ref, logits_ref,
    tok, nrm, own_tok, wz, wy, wo, act, acc_z, acc_y, proj, att, own_part,
    part_out, part_in, hid, col_sum, row_tile, pool_tile, pool_wide, pool_rows, bias_row, hidden_tile,
    local_sem, send_sem, recv_sem, tok_send, tok_recv, part_send, part_recv, pool_send, pool_recv,
):
    f = lax.axis_index("fsdp")
    s = lax.axis_index("seq")
    length = shards // PAIR
    a = f // PAIR
    b = f % PAIR
    rows = tok.shape[1]
    depth = nrm.shape[2]
    cols = wo.shape[2]
    z_cols = wz.shape[2]
    width = proj.shape[1] // 3
    heads = width // DH
    model = tok.shape[2]
    bufs = (wz, wy, wo)

    local = [
        pltpu.make_async_copy(tok_in, tok.at[0], local_sem.at[0]),
        pltpu.make_async_copy(
            qkv_in.at[0], wz.at[f, :, pl.ds(0, width)], local_sem.at[1]
        ),
        pltpu.make_async_copy(
            qkv_in.at[1], wz.at[f, :, pl.ds(width, width)], local_sem.at[2]
        ),
        pltpu.make_async_copy(
            qkv_in.at[2, :, pl.ds(0, z_cols - 2 * width)],
            wz.at[f, :, pl.ds(2 * width, z_cols - 2 * width)],
            local_sem.at[3],
        ),
        pltpu.make_async_copy(
            qkv_in.at[2, :, pl.ds(z_cols - 2 * width, wy.shape[2])], wy.at[f], local_sem.at[4]
        ),
        pltpu.make_async_copy(out_in, wo.at[f], local_sem.at[5]),
        pltpu.make_async_copy(act_in, act, local_sem.at[6]),
    ]
    hidden_copy = pltpu.make_async_copy(hidden_tile, hidden_ref, local_sem.at[7])
    for copy in local:
        copy.start()

    barrier = pltpu.get_barrier_semaphore()
    for k in range(1, shards):
        pl.semaphore_signal(barrier, inc=1, device_id={"fsdp": lax.rem(f + k, shards)},
                            device_id_type=pl.DeviceIdType.MESH)
    for k in range(1, seqs):
        pl.semaphore_signal(barrier, inc=1, device_id={"seq": lax.rem(s + k, seqs)},
                            device_id_type=pl.DeviceIdType.MESH)

    def shard_copy(kind, origin, way):
        if way == UP:
            target = lax.rem(f + PAIR, shards)
        elif way == DOWN:
            target = lax.rem(f + shards - PAIR, shards)
        else:
            target = a * PAIR + (1 - b)
        return pltpu.make_async_remote_copy(
            src_ref=bufs[kind].at[origin],
            dst_ref=bufs[kind].at[origin],
            send_sem=send_sem.at[way, kind, origin],
            recv_sem=recv_sem.at[kind, origin],
            device_id={"fsdp": target},
            device_id_type=pl.DeviceIdType.MESH,
        )

    def arrived(kind, origin):
        shard_copy(kind, origin, ACROSS).wait_recv()

    def send_up(kind, origin):
        @pl.when(a < length - 1)
        def _():
            shard_copy(kind, origin, UP).start()

    def send_down(kind, origin):
        @pl.when(a > 0)
        def _():
            shard_copy(kind, origin, DOWN).start()

    def at_distance(d, act_on):
        @pl.when(a - d >= 0)
        def _():
            act_on(0, a - d)

        @pl.when(jnp.logical_and(a + d < length, d > 0))
        def _():
            act_on(1, a + d)

    def tok_copy(k):
        return pltpu.make_async_remote_copy(
            src_ref=tok.at[0],
            dst_ref=tok.at[seqs - k],
            send_sem=tok_send.at[k],
            recv_sem=tok_recv.at[seqs - k],
            device_id={"seq": lax.rem(s + k, seqs)},
            device_id_type=pl.DeviceIdType.MESH,
        )

    for copy in local[:6]:
        copy.wait()
    pl.semaphore_wait(barrier, shards - 1 + seqs - 1)

    shard_copy(PAIR_QKV, f, ACROSS).start()
    shard_copy(LINE_QKV, f, ACROSS).start()
    send_up(LINE_QKV, f)
    send_down(LINE_QKV, f)
    for k in range(1, seqs):
        tok_copy(k).start()

    def norm_slot(k):
        step = 32

        def piece(i, carry):
            part = pl.ds(pl.multiple_of(i * step, step), step)
            values = normalize(tok[k, part, :].astype(F32)).astype(BF16)
            dest = pl.ds(pl.multiple_of(k * rows + i * step, step), step)
            for g in range(shards):
                nrm[g, dest, :] = values[:, g * depth:(g + 1) * depth]
            return carry

        lax.fori_loop(0, rows // step, piece, 0)

    norm_slot(0)
    for g in range(shards):
        own_tok[g] = tok[0, :, g * cols:(g + 1) * cols]
    table = table_ref[...]
    bins = bias_ref.shape[1]
    onehot = (lax.broadcasted_iota(jnp.int32, (bins, table.shape[1]), 0) == table).astype(F32)
    bias_row[...] = jnp.dot(
        bias_ref[...], onehot, preferred_element_type=F32, precision=lax.Precision.HIGHEST
    )
    acc_z[...] = jnp.zeros_like(acc_z)
    acc_y[...] = jnp.zeros_like(acc_y)

    half = acc_z.shape[0] // 2

    def add_z(origin):
        def piece(i, carry):
            part = pl.ds(pl.multiple_of(i * half, half), half)
            acc_z[part, :] += jnp.dot(nrm[origin, part, :], wz[origin],
                                      preferred_element_type=F32)
            return carry

        lax.fori_loop(0, 2, piece, 0)

    def add_y(origin):
        acc_y[...] += jnp.dot(nrm[origin], wy[origin], preferred_element_type=F32)

    def line_forward(kind, d):
        def forward(side, o):
            origin = o * PAIR + b
            arrived(kind, origin)
            if side == 0:
                send_up(kind, origin)
            else:
                send_down(kind, origin)
            shard_copy(kind, origin, ACROSS).start()

        at_distance(d, forward)

    turn = max(length - 2, 1)

    def line_step(d, carry):
        line_forward(LINE_QKV, d)

        @pl.when(d == turn)
        def _():
            send_up(PAIR_QKV, f)
            send_down(PAIR_QKV, f)
            other = a * PAIR + (1 - b)
            arrived(PAIR_QKV, other)
            send_up(PAIR_QKV, other)
            send_down(PAIR_QKV, other)

        @pl.when(d == 1)
        def _():
            for k in range(1, seqs):
                tok_copy(seqs - k).wait_recv()
                norm_slot(k)
            add_z(f)

        at_distance(d, lambda side, o: add_z(o * PAIR + b))
        return carry

    lax.fori_loop(1, length, line_step, 0)
    shard_copy(LINE_OUT, f, ACROSS).start()

    add_y(f)
    add_y(a * PAIR + (1 - b))

    def across_z(d):
        def use(side, o):
            origin = o * PAIR + (1 - b)
            arrived(LINE_QKV, origin)
            add_z(origin)

        at_distance(d, use)

    def pair_step(d, carry):
        for column in (b, 1 - b):
            def forward(side, o):
                origin = o * PAIR + column
                arrived(PAIR_QKV, origin)
                if side == 0:
                    send_up(PAIR_QKV, origin)
                else:
                    send_down(PAIR_QKV, origin)

            at_distance(d, forward)

        @pl.when(d == turn)
        def _():
            send_up(LINE_OUT, f)
            send_down(LINE_OUT, f)

        def use(side, o):
            add_y(o * PAIR)
            add_y(o * PAIR + 1)

        at_distance(d, use)
        across_z(d - 1)
        return carry

    lax.fori_loop(1, length, pair_step, 0)
    across_z(length - 1)

    proj[:, 0:z_cols] = acc_z[...].astype(BF16)
    proj[:, z_cols:] = acc_y[...].astype(BF16)
    scale = 1.0 / math.sqrt(DH)

    def head_step(h, carry):
        start = h * DH
        query = proj[:, pl.ds(start, DH)]
        key = proj[:, pl.ds(width + start, DH)]
        value = proj[:, pl.ds(2 * width + start, DH)]
        total = None
        mixed = None
        for k in range(seqs):
            part = slice(k * rows, (k + 1) * rows)
            score = lax.dot_general(query, key[part], (((1,), (1,)), ((), ())),
                                    preferred_element_type=F32)
            keep = valid_ref[0, lax.rem(s + k, seqs)].astype(F32)
            weight = jnp.exp(score * scale) * keep
            part_total = jnp.sum(weight, axis=-1, keepdims=True)
            part_mixed = jnp.dot(weight.astype(BF16), value[part], preferred_element_type=F32)
            total = part_total if total is None else total + part_total
            mixed = part_mixed if mixed is None else mixed + part_mixed
        att[:, pl.ds(start, DH)] = (mixed / total).astype(BF16)
        return carry

    for h in range(heads):
        head_step(h, 0)

    def part_copy(k, block):
        return pltpu.make_async_remote_copy(
            src_ref=part_out.at[k - 1, block],
            dst_ref=part_in.at[seqs - k - 1, block],
            send_sem=part_send.at[k - 1, block],
            recv_sem=part_recv.at[seqs - k - 1, block],
            device_id={"seq": lax.rem(s + k, seqs)},
            device_id_type=pl.DeviceIdType.MESH,
        )

    def out_block(block):
        product = jnp.dot(att[...], wo[block], preferred_element_type=F32)
        for k in range(1, seqs):
            part_out[k - 1, block] = product[k * rows:(k + 1) * rows].astype(BF16)
        own_part[block] = product[0:rows]
        for k in range(1, seqs):
            part_copy(k, block).start()

    out_block(f)

    def across_out(d):
        def use(side, o):
            origin = o * PAIR + (1 - b)
            arrived(LINE_OUT, origin)
            out_block(origin)

        at_distance(d, use)

    def finish(block):
        total = own_part[block]
        for k in range(1, seqs):
            part_copy(seqs - k, block).wait_recv()
            total = total + part_in[k - 1, block].astype(F32)
        rounded = (own_tok[block].astype(F32) + total).astype(BF16)
        hid[block] = rounded
        col_sum[block] = jnp.sum(rounded.astype(F32), axis=0, keepdims=True)

    def finish_at(d, column):
        at_distance(d, lambda side, o: finish(o * PAIR + column))

    def out_step(d, carry):
        line_forward(LINE_OUT, d)
        at_distance(d, lambda side, o: out_block(o * PAIR + b))
        finish_at(d - 1, b)

        @pl.when(d >= 2)
        def _():
            finish_at(d - 2, 1 - b)

        across_out(d - 1)
        return carry

    lax.fori_loop(1, length, out_step, 0)
    finish_at(length - 1, b)
    finish_at(length - 2, 1 - b)
    across_out(length - 1)
    finish_at(length - 1, 1 - b)


    pooled = normalize(
        jnp.concatenate([col_sum[g] for g in range(shards)], axis=-1) * (1.0 / rows)
    )
    lanes = row_tile.shape[1]
    for i in range(model // lanes):
        row_tile[i:i + 1, :] = pooled[:, i * lanes:(i + 1) * lanes]
    pool_tile[f] = row_tile[...].astype(BF16)

    def pool_copy(k):
        target = lax.rem(f + k, shards)
        return pltpu.make_async_remote_copy(
            src_ref=pool_tile.at[f],
            dst_ref=pool_tile.at[f],
            send_sem=pool_send.at[k],
            recv_sem=pool_recv.at[k],
            device_id={"fsdp": target},
            device_id_type=pl.DeviceIdType.MESH,
        )

    for k in range(1, shards):
        pool_copy(k).start()
    for g in range(shards):
        hidden_tile[:, g * cols:(g + 1) * cols] = hid[g]
    hidden_copy.start()
    local[6].wait()

    for k in range(1, seqs):
        tok_copy(k).wait_send()

    def drain(o, carry):
        own = o * PAIR + b
        other = o * PAIR + (1 - b)
        for kind in (LINE_QKV, LINE_OUT):
            shard_copy(kind, own, ACROSS).wait_send()

        @pl.when(jnp.logical_and(o <= a, a < length - 1))
        def _():
            for kind in (LINE_QKV, LINE_OUT, PAIR_QKV):
                shard_copy(kind, own, UP).wait_send()
            shard_copy(PAIR_QKV, other, UP).wait_send()

        @pl.when(jnp.logical_and(o >= a, a > 0))
        def _():
            for kind in (LINE_QKV, LINE_OUT, PAIR_QKV):
                shard_copy(kind, own, DOWN).wait_send()
            shard_copy(PAIR_QKV, other, DOWN).wait_send()

        return carry

    lax.fori_loop(0, length, drain, 0)
    shard_copy(PAIR_QKV, f, ACROSS).wait_send()

    def drain_parts(block, carry):
        for k in range(1, seqs):
            part_copy(k, block).wait_send()
        return carry

    lax.fori_loop(0, shards, drain_parts, 0)

    for k in range(1, shards):
        pool_copy(k).wait_recv()
    pool_wide[...] = pool_tile[...].astype(F32)
    for i in range(model // lanes):
        pool_rows[:, i * lanes:(i + 1) * lanes] = pool_wide[:, i, :]
    logits = (
        jnp.dot(pool_rows[...].astype(BF16), act[...], preferred_element_type=F32)
        + bias_row[...]
    )
    for g in range(shards):
        logits_ref[g] = logits[g:g + 1]
    for k in range(1, shards):
        pool_copy(k).wait_send()
    hidden_copy.wait()


def per_device(shards, seqs, tokens, frame_valid, w_qkv, w_out, w_act, class_table, cam_bias):
    rows, model = tokens.shape[3], tokens.shape[4]
    depth, width = w_qkv.shape[0], w_qkv.shape[2]
    cols, classes = w_out.shape[1], w_act.shape[1]
    span = seqs * rows
    y_cols = width // 2
    z_cols = 3 * width - y_cols
    lanes = 128
    any_spec = pl.BlockSpec(memory_space=pl.ANY)
    vmem_spec = pl.BlockSpec(memory_space=pltpu.VMEM)
    hidden, logits = pl.pallas_call(
        functools.partial(layer_kernel, shards, seqs),
        out_shape=(
            jax.ShapeDtypeStruct((rows, model), BF16),
            jax.ShapeDtypeStruct((shards, 1, classes), F32),
        ),
        in_specs=[
            any_spec,
            pl.BlockSpec(memory_space=pltpu.SMEM),
            any_spec, any_spec, any_spec, vmem_spec, vmem_spec,
        ],
        out_specs=(any_spec, vmem_spec),
        scratch_shapes=[
            pltpu.VMEM((seqs, rows, model), BF16),
            pltpu.VMEM((shards, span, depth), BF16),
            pltpu.VMEM((shards, rows, cols), BF16),
            pltpu.VMEM((shards, depth, z_cols), BF16),
            pltpu.VMEM((shards, depth, y_cols), BF16),
            pltpu.VMEM((shards, width, cols), BF16),
            pltpu.VMEM((model, classes), BF16),
            pltpu.VMEM((span, z_cols), F32),
            pltpu.VMEM((span, y_cols), F32),
            pltpu.VMEM((span, 3 * width), BF16),
            pltpu.VMEM((span, width), BF16),
            pltpu.VMEM((shards, rows, cols), F32),
            pltpu.VMEM((seqs - 1, shards, rows, cols), BF16),
            pltpu.VMEM((seqs - 1, shards, rows, cols), BF16),
            pltpu.VMEM((shards, rows, cols), BF16),
            pltpu.VMEM((shards, 1, cols), F32),
            pltpu.VMEM((model // lanes, lanes), F32),
            pltpu.VMEM((shards, model // lanes, lanes), BF16),
            pltpu.VMEM((shards, model // lanes, lanes), F32),
            pltpu.VMEM((shards, model), F32),
            pltpu.VMEM((1, classes), F32),
            pltpu.VMEM((rows, model), BF16),
            pltpu.SemaphoreType.DMA((8,)),
            pltpu.SemaphoreType.DMA((3, 3, shards)),
            pltpu.SemaphoreType.DMA((3, shards)),
            pltpu.SemaphoreType.DMA((seqs,)),
            pltpu.SemaphoreType.DMA((seqs,)),
            pltpu.SemaphoreType.DMA((seqs - 1, shards)),
            pltpu.SemaphoreType.DMA((seqs - 1, shards)),
            pltpu.SemaphoreType.DMA((shards,)),
            pltpu.SemaphoreType.DMA((shards,)),
        ],
        compiler_params=pltpu.CompilerParams(
            collective_id=0, has_side_effects=True, vmem_limit_bytes=60 * 1024 * 1024
        ),
        name="layer",
    )(
        tokens.reshape(rows, model),
        frame_valid.reshape(1, seqs),
        jnp.transpose(w_qkv, (1, 0, 2)),
        w_out,
        w_act,
        class_table.reshape(1, classes),
        cam_bias.reshape(1, cam_bias.shape[0]),
    )
    return (
        hidden.reshape(1, 1, 1, rows, model),
        logits.reshape(shards, 1, 1, classes),
    )


def solution(mesh):
    in_specs = (
        P(("groups", "fsdp"), "sub", "seq", None, None),
        P(("groups", "fsdp"), "sub", None),
        P("fsdp", None, "seq"),
        P("seq", "fsdp"),
        P(None, "fsdp"),
        P("fsdp"),
        P(),
    )
    out_specs = (P(("groups", "fsdp"), "sub", "seq", None, None), P("groups", "sub", "seq", "fsdp"))
    body = functools.partial(per_device, mesh.shape["fsdp"], mesh.shape["seq"])
    return jax.shard_map(
        body, mesh=mesh, in_specs=in_specs, out_specs=out_specs, check_vma=False
    )
```
